32 devices in a mesh: dp: 4 (over y, core), ulysses: 2 (over x), blk: 4 (over z).
Axes of the slice: x: 2, y: 2, z: 4, core: 2. Of those that a mesh axis runs over, the one named last changes fastest.
Arguments:
- tokens: bfloat16 [2, 2048, 2560], P(None, ('dp', 'ulysses', 'blk')), may hold values from -6 to 6
- segments: int32 [2, 2048], P(None, ('dp', 'ulysses', 'blk')), may hold values from 0 to 3, never falling along the last dimension, each value on 1 to 2000 neighbouring positions
- norm1: bfloat16 [2560], P(('dp', 'ulysses', 'blk')), may hold values from 0.099609375 to 1.8984375
- wq: bfloat16 [2560, 2560], P(('dp', 'ulysses'), 'blk'), may hold values from -0.125 to 0.125
- wk: bfloat16 [2560, 640], P(('dp', 'ulysses'), 'blk'), may hold values from -0.125 to 0.125
- wv: bfloat16 [2560, 640], P(('dp', 'ulysses'), 'blk'), may hold values from -0.125 to 0.125
- wo: bfloat16 [2560, 2560], P(('dp', 'ulysses'), 'blk'), may hold values from -1 to 1
- norm2: bfloat16 [2560], P(('dp', 'ulysses', 'blk')), may hold values from 0.099609375 to 1.8984375
- w_gate: bfloat16 [2560, 7168], P(('dp', 'ulysses'), 'blk'), may hold values from -0.125 to 0.125
- w_up: bfloat16 [2560, 7168], P(('dp', 'ulysses'), 'blk'), may hold values from -0.125 to 0.125
- w_down: bfloat16 [7168, 2560], P(('dp', 'ulysses'), 'blk'), may hold values from -0.0625 to 0.0625
- cotangent: bfloat16 [2, 2048, 2560], P(None, ('dp', 'ulysses', 'blk')), may hold values from -6 to 6
Outputs:
- out: bfloat16 [2, 2048, 2560], P(None, ('dp', 'ulysses', 'blk'))
- d_input: float32 [2, 2048, 2560], P(None, ('dp', 'ulysses', 'blk'))
- grad_norm1: float32 [2560], P(('dp', 'ulysses', 'blk'))
- grad_wq: float32 [2560, 2560], P(('dp', 'ulysses'), 'blk')
- grad_wk: float32 [2560, 640], P(('dp', 'ulysses'), 'blk')
- grad_wv: float32 [2560, 640], P(('dp', 'ulysses'), 'blk')
- grad_wo: float32 [2560, 2560], P(('dp', 'ulysses'), 'blk')
- grad_norm2: float32 [2560], P(('dp', 'ulysses', 'blk'))
- grad_gate: float32 [2560, 7168], P(('dp', 'ulysses'), 'blk')
- grad_up: float32 [2560, 7168], P(('dp', 'ulysses'), 'blk')
- grad_down: float32 [7168, 2560], P(('dp', 'ulysses'), 'blk')
The draws below stay inside these ranges and needn't reach their ends.
Inputs may be any that keep to these rules, and one draw needn't show every extreme that they name: `segments`: along each row the numbers never fall; each of 0 to 3 takes one run of 1 to 2000 consecutive tokens, and one run has exactly 2000.
All inputs are finite; a program needn't handle non-finite values.
Results may differ from the reference program's by a relative error of at most 0.025.
Values may be sent and summed in bfloat16 or wider, within the bound.
No kernel may reach another device: no remote copies, remote signals or barrier semaphores. Data moves between devices by JAX's collectives and lax.ppermute only.
A program may use at most 832 MiB of HBM per device.

```python
import math
import jax
import jax.numpy as jnp
import numpy as np
from jax import lax

D = 2560
HEADS = 32
KV = 8
HD = 80
FF = 7168
MB = 2
MOST = 2000
QD = 2560
KVD = 640
SEQ = 512
ROWS = 2048
DOCS = 4
N_DP = 4


def steps_of(key, extent, split, smallest, largest):
    loudness, own = 1.0, jax.random.fold_in(key, 6)
    for axis_at, parts in split:
        heights = jnp.exp(jax.random.uniform(jax.random.fold_in(own, axis_at), (parts,), jnp.float32, smallest / len(split), largest / len(split)))
        loudness = loudness * jnp.repeat(heights, extent[axis_at] // parts).reshape([-1 if axis == axis_at else 1 for axis in range(len(extent))])
    return loudness


def length_profile(number_of, total, most, slope):
    loads = [(1 << 20) // math.isqrt(standing ** slope) + 1 for standing in range(2, number_of + 1)]
    spare, holding = total - most - (number_of - 1), [1] * (number_of - 1)
    while spare > 0:
        movable = [i for i in range(number_of - 1) if holding[i] < most]
        mass, budget = sum([loads[i] for i in movable]), spare
        for i in movable:
            more = min(most - holding[i], max(1, budget * loads[i] // mass), spare)
            holding[i] = holding[i] + more
            spare = spare - more
    return np.array([most] + holding)


def ragged(own_key, count, total, most, lean):
    if count == 2:
        one = jax.random.randint(own_key, (), max(1, total - most), min(most, total - 1) + 1)
        return jnp.stack([one, total - one])
    sizes = jnp.asarray(length_profile(count, total, most, lean), jnp.int32)
    twos = (count - 1) // 2
    giver, sink = sizes[1:1 + 2 * twos:2], sizes[2:2 + 2 * twos:2]
    margin = jnp.minimum(giver - 1, most - sink)
    moved = jax.random.randint(jax.random.fold_in(own_key, 1), (twos,), 0, 1 << 20) % (margin + 1)
    sizes = sizes.at[1:1 + 2 * twos:2].set(giver - moved).at[2:2 + 2 * twos:2].set(sink + moved)
    return sizes[jax.random.permutation(jax.random.fold_in(own_key, 2), count)]


def gaussian(own_key, shape, spread, most, split=(), kind=jnp.bfloat16):
    gain = steps_of(own_key, shape, split, -0.22, 0.18) if split else 1.0
    values = jax.random.normal(own_key, shape, jnp.float32) * spread * gain
    return jnp.minimum(jnp.maximum(values, -most), most).astype(kind)


def setup_inputs(seed: int = 0) -> dict:
    key_of = jax.random.split(jax.random.key(seed), 13)
    tokens = gaussian(key_of[0], (MB, ROWS, D), 1.0, 6.0, ((1, 32),))
    segments = jax.vmap(lambda own: jnp.searchsorted(jnp.cumsum(ragged(own, DOCS, ROWS, MOST, 1)), jnp.arange(ROWS), side="right"))(jax.random.split(key_of[1], MB)).reshape((MB, ROWS)).astype(jnp.int32)
    norm1 = jnp.clip(1.0 + 0.18 * jax.random.normal(key_of[2], (D,), jnp.float32), 0.099609375, 1.8984375).astype(jnp.bfloat16)
    wq = gaussian(key_of[3], (D, QD), D ** -0.5, 0.125, ((0, 8), (1, 4)))
    wk = gaussian(key_of[4], (D, KVD), D ** -0.5, 0.125, ((0, 8), (1, 4)))
    wv = gaussian(key_of[5], (D, KVD), D ** -0.5, 0.125, ((0, 8), (1, 4)))
    wo = gaussian(key_of[6], (QD, D), (QD // 64) ** -0.5, 1.0, ((0, 8), (1, 4)))
    norm2 = jnp.clip(1.0 + 0.18 * jax.random.normal(key_of[7], (D,), jnp.float32), 0.099609375, 1.8984375).astype(jnp.bfloat16)
    w_gate = gaussian(key_of[8], (D, FF), D ** -0.5, 0.125, ((0, 8), (1, 4)))
    w_up = gaussian(key_of[9], (D, FF), D ** -0.5, 0.125, ((0, 8), (1, 4)))
    w_down = gaussian(key_of[10], (FF, D), FF ** -0.5, 0.0625, ((0, 8), (1, 4)))
    cotangent = gaussian(key_of[11], (MB, ROWS, D), 1.0, 6.0, ((1, 32),))
    return dict(tokens=tokens, segments=segments, norm1=norm1, wq=wq, wk=wk, wv=wv, wo=wo, norm2=norm2, w_gate=w_gate, w_up=w_up, w_down=w_down, cotangent=cotangent)


@jax.custom_vjp
def low(v):
    return lax.optimization_barrier(v.astype(jnp.bfloat16)).astype(jnp.float32)

@jax.custom_vjp
def low_back(v):
    return v

def low_keep(v):
    return (low(v), None)

def low_pass(kept, grad):
    return (grad,)

def back_keep(v):
    return (v, None)

def back_low(kept, grad):
    return (low(grad),)
low.defvjp(low_keep, low_pass)
low_back.defvjp(back_keep, back_low)
epsilon = 1e-05
rope_base = 1000000.0
masked_score = -1e+30
highest = lax.Precision.HIGHEST

def product(left, right):
    return jnp.dot(left, right, precision=highest, preferred_element_type=jnp.float32)

def inverse_norm(values):
    return lax.rsqrt(lax.optimization_barrier(jnp.mean(values * values, axis=-1, keepdims=True)) + epsilon)

def rotate(field, positions, direction):
    half_width = field.shape[-1] // 2
    inverse_freq = rope_base ** (-2.0 * jnp.arange(half_width, dtype=jnp.float32) / field.shape[-1])
    angles = positions.astype(jnp.float32)[:, None] * inverse_freq[None, :]
    cosine = jnp.cos(angles)[:, None, :]
    sine_part = direction * jnp.sin(angles)[:, None, :]
    first_half = field[..., :half_width]
    second = field[..., half_width:]
    return jnp.concatenate([first_half * cosine - second * sine_part, second * cosine + first_half * sine_part], axis=-1)

def positions_of(seq_seg):
    onehot = (seq_seg[:, :, None] == jnp.arange(DOCS, dtype=jnp.int32)[None, None, :]).astype(jnp.int32)
    counts = lax.optimization_barrier(jnp.sum(onehot, axis=1)).astype(jnp.int32)
    starts = (jnp.cumsum(counts, axis=1) - counts).astype(jnp.int32)
    earlier = lax.optimization_barrier(jnp.sum(onehot * starts[:, None, :], axis=2)).astype(jnp.int32)
    return jnp.arange(seq_seg.shape[1], dtype=jnp.int32)[None, :] - earlier

def head_group(query_group, key_head, value_head, visible):
    scores = low_back(jnp.einsum('gqd,kd->gqk', query_group, key_head, precision=highest) * HD ** (-0.5))
    scores = jnp.where(visible[None], scores, masked_score)
    probabilities = jax.nn.softmax(scores, axis=-1)
    return jnp.einsum('gqk,kd->gqd', low(probabilities), value_head, precision=highest)

def one_sequence(query, key, value, seq_ids):
    length = seq_ids.shape[0]
    order = jnp.arange(length, dtype=jnp.int32)
    visible = (seq_ids[:, None] == seq_ids[None, :]) & (order[None, :] <= order[:, None])
    grouped = query.reshape(length, KV, HEADS // KV, HD).transpose(1, 2, 0, 3)
    key_heads = key.transpose(1, 0, 2)
    value_heads = value.transpose(1, 0, 2)
    checked = jax.checkpoint(head_group)

    def per_group(sliced):
        return checked(sliced[0], sliced[1], sliced[2], visible)
    attended = lax.map(per_group, (grouped, key_heads, value_heads))
    return attended.transpose(2, 0, 1, 3).reshape(length, HEADS * HD)

def forward(floats, gain1, weight_q, weight_k, weight_v, weight_o, gain2, weight_gate, weight_up, weight_down, positions, seq_seg):
    batch_count, row_count, model_width = floats.shape
    flat = floats.reshape(batch_count * row_count, model_width)
    token_count = flat.shape[0]
    flat_positions = positions.reshape(token_count)
    unit1 = flat * inverse_norm(flat)
    normed1 = low(unit1 * gain1)
    query = low_back(product(normed1, weight_q))
    key = low_back(product(normed1, weight_k))
    value = low_back(product(normed1, weight_v))
    query = low(rotate(query.reshape(token_count, HEADS, HD), flat_positions, 1.0))
    key = low(rotate(key.reshape(token_count, KV, HD), flat_positions, 1.0))
    value = low(value)
    seq_count = token_count // SEQ

    def per_sequence(running, sliced):
        return (running, one_sequence(sliced[0], sliced[1], sliced[2], sliced[3]))
    unused, attended = lax.scan(per_sequence, jnp.zeros((), jnp.float32), (query.reshape(seq_count, SEQ, HEADS, HD), key.reshape(seq_count, SEQ, KV, HD), value.reshape(seq_count, SEQ, KV * HD).reshape(seq_count, SEQ, KV, HD), seq_seg))
    attended = low_back(low(attended.reshape(token_count, HEADS * HD)))
    middle = flat + low_back(product(attended, weight_o))
    unit2 = middle * inverse_norm(middle)
    normed2 = low(unit2 * gain2)
    gate_proj = low_back(product(normed2, weight_gate))
    up_proj = low_back(product(normed2, weight_up))
    hidden = low(jax.nn.silu(gate_proj) * up_proj)
    result = middle + low_back(product(hidden, weight_down))
    return result.reshape(batch_count, row_count, model_width)

def reference(tokens, segments, norm1, wq, wk, wv, wo, norm2, w_gate, w_up, w_down, cotangent):
    seq_seg = segments.reshape(MB * N_DP, SEQ)
    positions = positions_of(seq_seg).reshape(MB, N_DP * SEQ)
    floats = [array.astype(jnp.float32) for array in (tokens, norm1, wq, wk, wv, wo, norm2, w_gate, w_up, w_down)]

    def run(floats_in, gain1, weight_q, weight_k, weight_v, weight_o, gain2, weight_gate, weight_up, weight_down):
        return forward(floats_in, gain1, weight_q, weight_k, weight_v, weight_o, gain2, weight_gate, weight_up, weight_down, positions, seq_seg)
    result, pullback = jax.vjp(run, *floats)
    grads = pullback(cotangent.astype(jnp.float32))
    return (result.astype(jnp.bfloat16), grads[0], grads[1], grads[2], grads[3], grads[4], grads[5], grads[6], grads[7], grads[8], grads[9])
```

```python
import functools
import math

import jax
import jax.numpy as jnp
from jax import lax
from jax.experimental import pallas as pl
from jax.experimental.pallas import tpu as pltpu
from jax.sharding import PartitionSpec as P

HD = 80


epsilon = 1e-05
rope_base = 1000000.0
masked_score = -1e30
key_width = 512
gain_block = 128


def inverse_norm(values):
    return lax.rsqrt(jnp.mean(values * values, axis=-1, keepdims=True) + epsilon)


def norm_back(grad_normed, gain_full, unit_rows, inverse):
    scaled = grad_normed * gain_full
    return inverse * (scaled - unit_rows * jnp.mean(scaled * unit_rows, axis=-1, keepdims=True))


def rotate(field, positions, direction):
    half_width = field.shape[-1] // 2
    inverse_freq = rope_base ** (-2.0 * jnp.arange(half_width, dtype=jnp.float32) / field.shape[-1])
    angles = positions.astype(jnp.float32)[:, None] * inverse_freq[None, :]
    cosine = jnp.cos(angles)[:, None, :]
    sine_part = direction * jnp.sin(angles)[:, None, :]
    first_half = field[..., :half_width]
    second = field[..., half_width:]
    return jnp.concatenate(
        [first_half * cosine - second * sine_part, second * cosine + first_half * sine_part],
        axis=-1,
    )


def gather_layer(norm1, wq, wk, wv, wo, norm2, w_gate, w_up, w_down):
    gain_a, query_w, key_w, value_w, out_w, gain_b, gate_w, up_w, down_w = (
        lax.all_gather(norm1, "blk", axis=0, tiled=True),
        lax.all_gather(wq, "blk", axis=1, tiled=True),
        lax.all_gather(wk, "blk", axis=1, tiled=True),
        lax.all_gather(wv, "blk", axis=1, tiled=True),
        lax.all_gather(wo, "blk", axis=1, tiled=True),
        lax.all_gather(norm2, "blk", axis=0, tiled=True),
        lax.all_gather(w_gate, "blk", axis=1, tiled=True),
        lax.all_gather(w_up, "blk", axis=1, tiled=True),
        lax.all_gather(w_down, "blk", axis=1, tiled=True),
    )
    return (
        lax.all_gather(gain_a, ("dp", "ulysses"), axis=0, tiled=True),
        lax.all_gather(query_w, ("dp", "ulysses"), axis=0, tiled=True),
        lax.all_gather(key_w, ("dp", "ulysses"), axis=0, tiled=True),
        lax.all_gather(value_w, ("dp", "ulysses"), axis=0, tiled=True),
        lax.all_gather(out_w, ("dp", "ulysses"), axis=0, tiled=True),
        lax.all_gather(gain_b, ("dp", "ulysses"), axis=0, tiled=True),
        lax.all_gather(gate_w, ("dp", "ulysses"), axis=0, tiled=True),
        lax.all_gather(up_w, ("dp", "ulysses"), axis=0, tiled=True),
        lax.all_gather(down_w, ("dp", "ulysses"), axis=0, tiled=True),
    )


def query_layout(seq_seg, tok_rows, part_count):
    part_len = seq_seg.shape[0] // part_count
    offset = lax.axis_index("blk") * tok_rows
    local_index = jnp.arange(tok_rows, dtype=jnp.int32)
    query_index = (
        jnp.arange(part_count, dtype=jnp.int32)[:, None] * part_len + offset + local_index[None, :]
    )
    query_seg = lax.dynamic_slice_in_dim(seq_seg.reshape(part_count, part_len), offset, tok_rows, 1)
    return (query_index, query_seg)


def visibility(seq_seg, query_index, query_seg, block_start, key_count):
    key_index = block_start + jnp.arange(key_count, dtype=jnp.int32)
    key_seg = lax.dynamic_slice_in_dim(seq_seg, block_start, key_count)
    return (key_seg[None, :] == query_seg[:, None]) & (key_index[None, :] <= query_index[:, None])


def keep_state(stats_in):
    return stats_in


def forward_block(query_part, key_block, value_block, visible, score_scale):

    def update(stats_in):
        running_max, running_sum, running_acc = stats_in
        scores = (
            jnp.einsum("qkgd,jkd->kgqj", query_part, key_block, preferred_element_type=jnp.float32)
            * score_scale
        )
        scores = jnp.where(visible[None, None], scores, masked_score)
        new_max = jnp.maximum(running_max, jnp.max(scores, axis=-1))
        weights = jnp.where(visible[None, None], jnp.exp(scores - new_max[..., None]), 0.0)
        shrink = jnp.exp(running_max - new_max)
        new_sum = running_sum * shrink + jnp.sum(weights, axis=-1)
        new_acc = running_acc * shrink[..., None] + jnp.einsum(
            "kgqj,jkd->kgqd",
            weights.astype(jnp.bfloat16),
            value_block,
            preferred_element_type=jnp.float32,
        )
        return (new_max, new_sum, new_acc)

    return update


def backward_block(
    query_part, grad_part, key_block, value_block, visible, log_sum, delta, score_scale
):

    def update(grads_in):
        grad_query, grad_key, grad_value = grads_in
        scores = (
            jnp.einsum("qkgd,jkd->kgqj", query_part, key_block, preferred_element_type=jnp.float32)
            * score_scale
        )
        probabilities = jnp.where(visible[None, None], jnp.exp(scores - log_sum[..., None]), 0.0)
        grad_value = grad_value + jnp.einsum(
            "kgqj,qkgd->jkd",
            probabilities.astype(jnp.bfloat16),
            grad_part,
            preferred_element_type=jnp.float32,
        )
        grad_probs = jnp.einsum(
            "qkgd,jkd->kgqj", grad_part, value_block, preferred_element_type=jnp.float32
        )
        grad_scores = (probabilities * (grad_probs - delta[..., None])).astype(jnp.bfloat16)
        grad_query = grad_query + score_scale * jnp.einsum(
            "kgqj,jkd->kgqd", grad_scores, key_block, preferred_element_type=jnp.float32
        )
        grad_key = grad_key + score_scale * jnp.einsum(
            "kgqj,qkgd->jkd", grad_scores, query_part, preferred_element_type=jnp.float32
        )
        return (grad_query, grad_key, grad_value)

    return update


def attend_forward(queries, keys, values, seq_seg, query_index, query_seg):
    part_count, tok_rows, kv_local, group_size, head_dim = queries.shape
    seq_len = keys.shape[0]
    key_count = math.gcd(key_width, seq_len // part_count)
    score_scale = head_dim ** (-0.5)

    def scan_step(running, block_index):
        block_start = block_index * key_count
        key_block = lax.dynamic_slice_in_dim(keys, block_start, key_count, 0)
        value_block = lax.dynamic_slice_in_dim(values, block_start, key_count, 0)
        updated = []
        for part_index in range(part_count):
            visible = visibility(
                seq_seg, query_index[part_index], query_seg[part_index], block_start, key_count
            )
            update = forward_block(
                queries[part_index], key_block, value_block, visible, score_scale
            )
            updated.append(lax.cond(jnp.any(visible), update, keep_state, running[part_index]))
        return (tuple(updated), None)

    initial = tuple(
        (
            (
                jnp.full((kv_local, group_size, tok_rows), masked_score, jnp.float32),
                jnp.zeros((kv_local, group_size, tok_rows), jnp.float32),
                jnp.zeros((kv_local, group_size, tok_rows, head_dim), jnp.float32),
            )
            for part_index in range(part_count)
        )
    )
    finished, unused = lax.scan(
        scan_step, initial, jnp.arange(seq_len // key_count, dtype=jnp.int32)
    )
    outputs = jnp.stack([part_stats[2] / part_stats[1][..., None] for part_stats in finished])
    log_sums = jnp.stack([part_stats[0] + jnp.log(part_stats[1]) for part_stats in finished])
    return (outputs, log_sums)


def attend_backward(
    queries, keys, values, seq_seg, query_index, query_seg, grad_out, outputs, log_sums
):
    part_count, tok_rows, kv_local, group_size, head_dim = queries.shape
    seq_len = keys.shape[0]
    key_count = math.gcd(key_width, seq_len // part_count)
    score_scale = head_dim ** (-0.5)
    delta_all = jnp.einsum("pqkgd,pkgqd->pkgq", grad_out.astype(jnp.float32), outputs)

    def scan_step(running, block_index):
        block_start = block_index * key_count
        key_block = lax.dynamic_slice_in_dim(keys, block_start, key_count, 0)
        value_block = lax.dynamic_slice_in_dim(values, block_start, key_count, 0)
        grad_key = jnp.zeros((key_count, kv_local, head_dim), jnp.float32)
        grad_value = jnp.zeros((key_count, kv_local, head_dim), jnp.float32)
        updated = []
        for part_index in range(part_count):
            visible = visibility(
                seq_seg, query_index[part_index], query_seg[part_index], block_start, key_count
            )
            update = backward_block(
                queries[part_index],
                grad_out[part_index],
                key_block,
                value_block,
                visible,
                log_sums[part_index],
                delta_all[part_index],
                score_scale,
            )
            grad_query, grad_key, grad_value = lax.cond(
                jnp.any(visible), update, keep_state, (running[part_index], grad_key, grad_value)
            )
            updated.append(grad_query)
        block_grads = jnp.concatenate(
            [
                grad_key.reshape(key_count, kv_local * head_dim),
                grad_value.reshape(key_count, kv_local * head_dim),
            ],
            axis=1,
        )
        return (tuple(updated), block_grads)

    initial = tuple(
        (
            jnp.zeros((kv_local, group_size, tok_rows, head_dim), jnp.float32)
            for part_index in range(part_count)
        )
    )
    finished, key_terms = lax.scan(
        scan_step, initial, jnp.arange(seq_len // key_count, dtype=jnp.int32)
    )
    return (
        jnp.stack(finished),
        key_terms.reshape(part_count, seq_len // part_count, 2 * kv_local * head_dim),
    )


def forward_batch(tokens, own_seg, seq_seg, attn_weights, ffn_weights):
    gain1, weight_q, weight_k, weight_v, weight_o = attn_weights
    gain2, weight_gate, weight_up, weight_down = ffn_weights
    tok_rows = tokens.shape[0]
    part_count = lax.axis_size("ulysses")
    head_count = weight_q.shape[1] // HD
    kv_count = weight_k.shape[1] // HD
    group_q = weight_q.shape[1] // part_count
    group_kv = weight_k.shape[1] // part_count
    seq_len = seq_seg.shape[0]
    block_id = lax.axis_index("ulysses") * lax.axis_size("blk") + lax.axis_index("blk")
    token_index = block_id * tok_rows + jnp.arange(tok_rows, dtype=jnp.int32)
    positions = token_index - jnp.sum(
        (seq_seg[None, :] < own_seg[:, None]).astype(jnp.int32), axis=1
    )
    floats = tokens.astype(jnp.float32)
    inverse1 = inverse_norm(floats)
    unit1 = floats * inverse1
    normed1 = (unit1 * gain1.astype(jnp.float32)).astype(jnp.bfloat16)
    query_raw = jnp.dot(normed1, weight_q, preferred_element_type=jnp.float32)
    key_raw = jnp.dot(normed1, weight_k, preferred_element_type=jnp.float32)
    value_raw = jnp.dot(normed1, weight_v, preferred_element_type=jnp.float32)
    query_rot = rotate(query_raw.reshape(tok_rows, head_count, HD), positions, 1.0).astype(
        jnp.bfloat16
    )
    key_rot = rotate(key_raw.reshape(tok_rows, kv_count, HD), positions, 1.0).astype(jnp.bfloat16)
    packed = jnp.concatenate(
        [
            query_rot.reshape(tok_rows, part_count, group_q),
            key_rot.reshape(tok_rows, part_count, group_kv),
            value_raw.astype(jnp.bfloat16).reshape(tok_rows, part_count, group_kv),
        ],
        axis=2,
    )
    arrived = lax.all_to_all(packed, "ulysses", split_axis=1, concat_axis=0, tiled=True)
    queries = arrived[:, 0, :group_q].reshape(
        part_count, tok_rows, kv_count // part_count, head_count // kv_count, HD
    )
    local_kv = arrived[:, 0, group_q:].reshape(part_count, tok_rows, 2 * group_kv)
    all_kv = lax.all_gather(local_kv, "blk", axis=1, tiled=True).reshape(seq_len, 2 * group_kv)
    keys = all_kv[:, :group_kv].reshape(seq_len, kv_count // part_count, HD)
    values = all_kv[:, group_kv:].reshape(seq_len, kv_count // part_count, HD)
    query_index, query_seg = query_layout(seq_seg, tok_rows, part_count)
    outputs, log_sums = attend_forward(queries, keys, values, seq_seg, query_index, query_seg)
    sending = (
        outputs.transpose(0, 3, 1, 2, 4)
        .reshape(part_count, tok_rows, 1, group_q)
        .astype(jnp.bfloat16)
    )
    attended = lax.all_to_all(sending, "ulysses", split_axis=0, concat_axis=2, tiled=True).reshape(
        tok_rows, part_count * group_q
    )
    middle = floats + jnp.dot(attended, weight_o, preferred_element_type=jnp.float32)
    inverse2 = inverse_norm(middle)
    unit2 = middle * inverse2
    normed2 = (unit2 * gain2.astype(jnp.float32)).astype(jnp.bfloat16)
    gate_proj = jnp.dot(normed2, weight_gate, preferred_element_type=jnp.float32)
    up_proj = jnp.dot(normed2, weight_up, preferred_element_type=jnp.float32)
    hidden = (jax.nn.silu(gate_proj) * up_proj).astype(jnp.bfloat16)
    result = (middle + jnp.dot(hidden, weight_down, preferred_element_type=jnp.float32)).astype(
        jnp.bfloat16
    )
    saved = (
        positions,
        inverse1,
        unit1,
        normed1,
        queries,
        keys,
        values,
        query_index,
        query_seg,
        outputs,
        log_sums,
        attended,
        inverse2,
        unit2,
        normed2,
        gate_proj,
        up_proj,
        hidden,
    )
    return (result, saved)


def backward_batch(cotan, seq_seg, saved, attn_weights, ffn_weights):
    (
        positions,
        inverse1,
        unit1,
        normed1,
        queries,
        keys,
        values,
        query_index,
        query_seg,
        outputs,
        log_sums,
        attended,
        inverse2,
        unit2,
        normed2,
        gate_proj,
        up_proj,
        hidden,
    ) = saved
    gain1, weight_q, weight_k, weight_v, weight_o = attn_weights
    gain2, weight_gate, weight_up, weight_down = ffn_weights
    tok_rows = cotan.shape[0]
    part_count = lax.axis_size("ulysses")
    head_count = weight_q.shape[1] // HD
    kv_count = weight_k.shape[1] // HD
    group_q = weight_q.shape[1] // part_count
    group_kv = weight_k.shape[1] // part_count
    grad_hidden = jnp.einsum("td,fd->tf", cotan, weight_down, preferred_element_type=jnp.float32)
    gate_sigmoid = jax.nn.sigmoid(gate_proj)
    grad_gate = (
        grad_hidden * up_proj * gate_sigmoid * (1.0 + gate_proj * (1.0 - gate_sigmoid))
    ).astype(jnp.bfloat16)
    grad_up = (grad_hidden * gate_proj * gate_sigmoid).astype(jnp.bfloat16)
    grad_normed2 = jnp.einsum(
        "tf,df->td", grad_gate, weight_gate, preferred_element_type=jnp.float32
    ) + jnp.einsum("tf,df->td", grad_up, weight_up, preferred_element_type=jnp.float32)
    grad_middle = cotan.astype(jnp.float32) + norm_back(
        grad_normed2, gain2.astype(jnp.float32), unit2, inverse2
    )
    grad_attn = grad_middle.astype(jnp.bfloat16)
    grad_attended = jnp.einsum(
        "td,qd->tq", grad_attn, weight_o, preferred_element_type=jnp.float32
    ).astype(jnp.bfloat16)
    grad_sent = lax.all_to_all(
        grad_attended.reshape(tok_rows, part_count, group_q),
        "ulysses",
        split_axis=1,
        concat_axis=0,
        tiled=True,
    )
    grad_out = grad_sent.reshape(queries.shape)
    grad_queries, key_terms = attend_backward(
        queries, keys, values, seq_seg, query_index, query_seg, grad_out, outputs, log_sums
    )
    key_sums = lax.psum_scatter(
        key_terms.astype(jnp.bfloat16), "blk", scatter_dimension=1, tiled=True
    ).astype(jnp.float32)
    back_pack = jnp.concatenate(
        [grad_queries.transpose(0, 3, 1, 2, 4).reshape(part_count, tok_rows, group_q), key_sums],
        axis=2,
    )[:, :, None, :]
    returned = (
        lax.all_to_all(
            back_pack.astype(jnp.bfloat16), "ulysses", split_axis=0, concat_axis=2, tiled=True
        )
        .astype(back_pack.dtype)
        .reshape(tok_rows, part_count, group_q + 2 * group_kv)
    )
    grad_query = (
        rotate(returned[:, :, :group_q].reshape(tok_rows, head_count, HD), positions, -1.0)
        .reshape(tok_rows, head_count * HD)
        .astype(jnp.bfloat16)
    )
    grad_key = (
        rotate(
            returned[:, :, group_q : group_q + group_kv].reshape(tok_rows, kv_count, HD),
            positions,
            -1.0,
        )
        .reshape(tok_rows, kv_count * HD)
        .astype(jnp.bfloat16)
    )
    grad_value = (
        returned[:, :, group_q + group_kv :].reshape(tok_rows, kv_count * HD).astype(jnp.bfloat16)
    )
    grad_normed1 = (
        jnp.einsum("tq,dq->td", grad_query, weight_q, preferred_element_type=jnp.float32)
        + jnp.einsum("tk,dk->td", grad_key, weight_k, preferred_element_type=jnp.float32)
        + jnp.einsum("tk,dk->td", grad_value, weight_v, preferred_element_type=jnp.float32)
    )
    grad_input = grad_middle + norm_back(grad_normed1, gain1.astype(jnp.float32), unit1, inverse1)
    pieces = (
        normed1,
        jnp.concatenate([grad_query, grad_key, grad_value], axis=1),
        attended,
        grad_attn,
        unit1,
        grad_normed1,
        normed2,
        jnp.concatenate([grad_gate, grad_up], axis=1),
        unit2,
        grad_normed2,
        hidden,
        cotan,
    )
    return (grad_input, pieces)


def gain_column(unit_rows, grad_normed, row_count):
    column = jnp.sum(unit_rows * grad_normed, axis=0)
    return jnp.concatenate(
        [column[:, None], jnp.zeros((row_count, gain_block - 1), jnp.float32)], axis=1
    )


def scatter_grads(pieces, width_q, width_kv, hidden_width):
    (
        normed1,
        grad_qkv,
        attended,
        grad_attn,
        unit1,
        grad_normed1,
        normed2,
        grad_gu,
        unit2,
        grad_normed2,
        hidden,
        cotan,
    ) = pieces
    model_width = normed1.shape[1]
    outer_count = lax.axis_size("dp") * lax.axis_size("ulysses")
    projections = jnp.einsum("tc,tk->ck", normed1, grad_qkv, preferred_element_type=jnp.float32)
    output_rows = jnp.einsum("tc,td->cd", attended, grad_attn, preferred_element_type=jnp.float32)
    feed_rows = jnp.einsum("tc,tk->ck", normed2, grad_gu, preferred_element_type=jnp.float32)
    row_part = lax.psum_scatter(
        jnp.concatenate(
            [
                projections,
                output_rows,
                gain_column(
                    unit1,
                    grad_normed1,
                    lax.axis_size(("dp", "ulysses")) * (model_width // outer_count),
                ),
                feed_rows,
                gain_column(
                    unit2,
                    grad_normed2,
                    lax.axis_size(("dp", "ulysses")) * (model_width // outer_count),
                ),
            ],
            axis=1,
        ).astype(jnp.bfloat16),
        ("dp", "ulysses"),
        scatter_dimension=0,
        tiled=True,
    ).astype(jnp.float32)
    down_part = lax.psum_scatter(
        jnp.einsum("tf,td->fd", hidden, cotan, preferred_element_type=jnp.float32).astype(
            jnp.bfloat16
        ),
        ("dp", "ulysses"),
        scatter_dimension=0,
        tiled=True,
    )
    start_o = width_q + 2 * width_kv
    start_gain1 = start_o + model_width
    start_ffn = start_gain1 + gain_block
    start_gain2 = start_ffn + 2 * hidden_width
    part_q = row_part[:, :width_q]
    part_k = row_part[:, width_q : width_q + width_kv]
    part_v = row_part[:, width_q + width_kv : start_o]
    part_o = row_part[:, start_o:start_gain1]
    part_gain1 = row_part[:, start_gain1]
    part_gate = row_part[:, start_ffn : start_ffn + hidden_width]
    part_up = row_part[:, start_ffn + hidden_width : start_gain2]
    part_gain2 = row_part[:, start_gain2]
    return (
        lax.psum_scatter(
            part_gain1.astype(jnp.bfloat16), "blk", scatter_dimension=0, tiled=True
        ).astype(jnp.float32),
        lax.psum_scatter(
            part_q.astype(jnp.bfloat16), "blk", scatter_dimension=1, tiled=True
        ).astype(jnp.float32),
        lax.psum_scatter(
            part_k.astype(jnp.bfloat16), "blk", scatter_dimension=1, tiled=True
        ).astype(jnp.float32),
        lax.psum_scatter(
            part_v.astype(jnp.bfloat16), "blk", scatter_dimension=1, tiled=True
        ).astype(jnp.float32),
        lax.psum_scatter(
            part_o.astype(jnp.bfloat16), "blk", scatter_dimension=1, tiled=True
        ).astype(jnp.float32),
        lax.psum_scatter(
            part_gain2.astype(jnp.bfloat16), "blk", scatter_dimension=0, tiled=True
        ).astype(jnp.float32),
        lax.psum_scatter(
            part_gate.astype(jnp.bfloat16), "blk", scatter_dimension=1, tiled=True
        ).astype(jnp.float32),
        lax.psum_scatter(
            part_up.astype(jnp.bfloat16), "blk", scatter_dimension=1, tiled=True
        ).astype(jnp.float32),
        lax.psum_scatter(down_part, "blk", scatter_dimension=1, tiled=True).astype(jnp.float32),
    )


def shards(tokens, segments, norm1, wq, wk, wv, wo, norm2, w_gate, w_up, w_down, cotangent):
    batch_count = tokens.shape[0]
    seq_seg = lax.all_gather(segments, ("ulysses", "blk"), axis=1, tiled=True)
    shared = gather_layer(norm1, wq, wk, wv, wo, norm2, w_gate, w_up, w_down)
    weight_sets = [shared for batch_index in range(batch_count)]
    results = []
    grad_inputs = []
    piece_lists = []
    for batch_index in range(batch_count):
        layer = weight_sets[batch_index]
        attn_weights = layer[:5]
        ffn_weights = layer[5:]
        result, saved = forward_batch(
            tokens[batch_index],
            segments[batch_index],
            seq_seg[batch_index],
            attn_weights,
            ffn_weights,
        )
        grad_input, pieces = backward_batch(
            cotangent[batch_index], seq_seg[batch_index], saved, attn_weights, ffn_weights
        )
        results.append(result)
        grad_inputs.append(grad_input)
        piece_lists.append(pieces)
    merged = tuple(
        (
            jnp.concatenate([pieces[slot_index] for pieces in piece_lists], axis=0)
            for slot_index in range(len(piece_lists[0]))
        )
    )
    full_layer = weight_sets[0]
    width_q = full_layer[1].shape[1]
    width_kv = full_layer[2].shape[1]
    hidden_width = full_layer[6].shape[1]
    grad_norm1, grad_wq, grad_wk, grad_wv, grad_wo, grad_norm2, grad_gate, grad_up, grad_down = (
        scatter_grads(merged, width_q, width_kv, hidden_width)
    )
    return (
        jnp.stack(results),
        jnp.stack(grad_inputs),
        grad_norm1,
        grad_wq,
        grad_wk,
        grad_wv,
        grad_wo,
        grad_norm2,
        grad_gate,
        grad_up,
        grad_down,
    )


def swap_pairs(count, bit):
    return [(index, index ^ bit) for index in range(count)]


def cube_gather(block, axes):
    for name in axes:
        count = lax.axis_size(name)
        bit = 1
        while bit < count:
            other = lax.ppermute(block, name, swap_pairs(count, bit))
            high = (lax.axis_index(name) & bit) != 0
            block = jnp.concatenate(
                [jnp.where(high, other, block), jnp.where(high, block, other)], axis=0
            )
            bit *= 2
    return block


def cube_scatter(values, axes):
    for name in axes:
        count = lax.axis_size(name)
        bit = count // 2
        while bit:
            half = values.shape[0] // 2
            high = (lax.axis_index(name) & bit) != 0
            low_half, high_half = values[:half], values[half:]
            sent = jnp.where(high, low_half, high_half)
            kept = jnp.where(high, high_half, low_half)
            values = kept + lax.ppermute(sent, name, swap_pairs(count, bit))
            bit //= 2
    return values


def ring_pairs(count, direction):
    return [(index, (index + direction) % count) for index in range(count)]


def ring_gather(parts):
    count = lax.axis_size("blk")
    slots = [[part] for part in parts]
    for step in range(count - 1):
        for m in range(len(parts)):
            slots[m].append(lax.ppermute(slots[m][-1], "blk", ring_pairs(count, direction_of(m))))
    return [jnp.concatenate(each, axis=0) for each in slots]


def ring_scatter(partials, rows):
    count = lax.axis_size("blk")

    def piece(m, slot):
        slot = slot % count
        return partials[m][slot * rows : (slot + 1) * rows]

    sums = [piece(m, 1) for m in range(len(partials))]
    for step in range(1, count):
        for m in range(len(partials)):
            arrived = lax.ppermute(
                sums[m].astype(jnp.bfloat16), "blk", ring_pairs(count, direction_of(m))
            )
            sums[m] = arrived.astype(jnp.float32) + piece(m, step + 1)
    return sums


def direction_of(m):
    return 1 if m % 2 == 0 else -1


def place_of(index, count):
    bits = count.bit_length() - 1
    return int(format(index, f"0{bits}b")[::-1], 2) if bits else 0


def cross_pairs(count):
    return [
        (d * count + z, place_of(z, count) * count + d) for d in range(count) for z in range(count)
    ]


def cross_back_pairs(count):
    return [(target, source) for source, target in cross_pairs(count)]


def turned(x_ref, padded, cosine, sine):
    width = x_ref.shape[-1]
    padded_width = padded.shape[-1]
    padded[:, :width] = x_ref[...].astype(jnp.float32)
    whole = padded[...]
    half = HD // 2
    lane = lax.broadcasted_iota(jnp.int32, whole.shape, 1)
    first = lax.rem(lane, HD) < half
    other = jnp.where(
        first,
        pltpu.roll(whole, padded_width - half, 1),
        pltpu.roll(whole, half, 1),
    )
    return padded[:, :width] * cosine + other[:, :width] * sine


def turn_kernel(direction, x_ref, cos_ref, sin_ref, out_ref, padded):
    out_ref[...] = turned(x_ref, padded, cos_ref[...], direction * sin_ref[...]).astype(
        out_ref.dtype
    )


def turn(values, cosine, sine, direction):
    rows, width = values.shape
    block = math.gcd(rows, 256)
    spec = pl.BlockSpec((block, width), lambda i: (i, 0))
    return pl.pallas_call(
        functools.partial(turn_kernel, direction),
        grid=(rows // block,),
        in_specs=[spec, spec, spec],
        out_specs=spec,
        out_shape=jax.ShapeDtypeStruct((rows, width), jnp.bfloat16),
        scratch_shapes=[pltpu.VMEM((block, pl.cdiv(width, 128) * 128), jnp.float32)],
        cost_estimate=pl.CostEstimate(
            flops=6 * rows * width, bytes_accessed=14 * rows * width, transcendentals=0
        ),
    )(values, cosine, sine)


def heads_of(ref, first, count):
    return jnp.concatenate(
        [ref[0, :, (first + h) * HD : (first + h + 1) * HD] for h in range(count)], axis=0
    )


def mask_of(start_ref, index_ref, key_ref):
    keys = key_ref[0]
    seen = (keys >= start_ref[0]) & (keys <= index_ref[0])
    return jnp.where(seen, 0.0, masked_score)


def dot_nt(left, right):
    return lax.dot_general(left, right, (((1,), (1,)), ((), ())), preferred_element_type=jnp.float32)


def dot_tn(left, right):
    return lax.dot_general(left, right, (((0,), (0,)), ((), ())), preferred_element_type=jnp.float32)


def attend_kernel(group, q_ref, k_ref, v_ref, start_ref, index_ref, key_ref, out_ref, log_ref):
    rows = q_ref.shape[1]
    kv_count = k_ref.shape[2] // HD
    mask = mask_of(start_ref, index_ref, key_ref)
    for kv in range(kv_count):
        key = k_ref[0, :, kv * HD : (kv + 1) * HD]
        value = v_ref[0, :, kv * HD : (kv + 1) * HD]
        for g in range(group):
            h = kv * group + g
            query = q_ref[0, :, h * HD : (h + 1) * HD]
            scores = dot_nt(query, key) * (HD**-0.5) + mask
            top = jnp.max(scores, axis=1, keepdims=True)
            weights = jnp.exp(scores - top)
            total = jnp.sum(weights, axis=1, keepdims=True)
            mixed = jnp.dot(
                weights.astype(jnp.bfloat16), value, preferred_element_type=jnp.float32
            )
            out_ref[0, :, h * HD : (h + 1) * HD] = (mixed / total).astype(out_ref.dtype)
            log_ref[0, :, h : h + 1] = top + jnp.log(total)


def attend_back_kernel(
    group,
    q_ref,
    k_ref,
    v_ref,
    start_ref,
    index_ref,
    key_ref,
    log_ref,
    grad_ref,
    gq_ref,
    gk_ref,
    gv_ref,
):
    kv_count = k_ref.shape[2] // HD
    scale = HD**-0.5
    mask = mask_of(start_ref, index_ref, key_ref)
    for kv in range(kv_count):
        key = k_ref[0, :, kv * HD : (kv + 1) * HD]
        value = v_ref[0, :, kv * HD : (kv + 1) * HD]
        grad_key = None
        grad_value = None
        for g in range(group):
            h = kv * group + g
            query = q_ref[0, :, h * HD : (h + 1) * HD]
            grad = grad_ref[0, :, h * HD : (h + 1) * HD]
            scores = dot_nt(query, key) * scale + mask
            probs = jnp.exp(scores - log_ref[0, :, h : h + 1])
            grad_probs = dot_nt(grad, value)
            delta = jnp.sum(probs * grad_probs, axis=1, keepdims=True)
            grad_scores = (probs * (grad_probs - delta)).astype(jnp.bfloat16)
            gq_ref[0, :, h * HD : (h + 1) * HD] = (
                jnp.dot(grad_scores, key, preferred_element_type=jnp.float32) * scale
            )
            key_term = dot_tn(grad_scores, query)
            value_term = dot_tn(probs.astype(jnp.bfloat16), grad)
            grad_key = key_term if grad_key is None else grad_key + key_term
            grad_value = value_term if grad_value is None else grad_value + value_term
        gk_ref[0, :, kv * HD : (kv + 1) * HD] = grad_key * scale
        gv_ref[0, :, kv * HD : (kv + 1) * HD] = grad_value


def whole_block(shape):
    return pl.BlockSpec((1,) + shape[1:], lambda m: (m,) + (0,) * (len(shape) - 1))


def attend_call(kernel, operands, outs, flops, exps):
    return pl.pallas_call(
        kernel,
        grid=(operands[0].shape[0],),
        in_specs=[whole_block(each.shape) for each in operands],
        out_specs=[whole_block(each.shape) for each in outs],
        out_shape=outs,
        cost_estimate=pl.CostEstimate(
            flops=flops,
            bytes_accessed=sum(each.size * each.dtype.itemsize for each in (*operands, *outs)),
            transcendentals=exps,
        ),
    )(*operands)


def matmul(left, right):
    return jnp.dot(left, right, preferred_element_type=jnp.float32)


def matmul_nt(left, right):
    return jnp.einsum("tc,dc->td", left, right, preferred_element_type=jnp.float32)


def grad_of(left, right):
    return jnp.einsum("tc,td->cd", left, right, preferred_element_type=jnp.float32).astype(
        jnp.bfloat16
    )


def split_shards(
    tokens, segments, norm1, wq, wk, wv, wo, norm2, w_gate, w_up, w_down, cotangent
):
    batch_count, tok_rows, width = tokens.shape
    n_dp, n_u, n_z = (lax.axis_size(name) for name in ("dp", "ulysses", "blk"))
    u_id, z_id = lax.axis_index("ulysses"), lax.axis_index("blk")
    bf16, f32 = jnp.bfloat16, jnp.float32
    outer = ("dp", "ulysses")
    part_len = n_z * tok_rows
    seq_len = n_u * part_len
    group_rows = batch_count * part_len
    q_width, kv_width = wq.shape[1], wk.shape[1]
    group = q_width // kv_width
    gain_rows = norm1.shape[0]
    block_of = [place_of(z, n_z) for z in range(n_z)]

    own_wo, own_down = (lax.ppermute(w, ("dp", "blk"), cross_pairs(n_z)) for w in (wo, w_down))
    qkv_w = lax.all_gather(jnp.concatenate([wq, wk, wv], axis=1), outer, axis=0, tiled=True)
    wo_all = lax.all_gather(own_wo, outer, axis=0, tiled=True)
    gate_w = lax.all_gather(w_gate, outer, axis=0, tiled=True)
    up_w = lax.all_gather(w_up, outer, axis=0, tiled=True)
    down_all = lax.all_gather(own_down, outer, axis=0, tiled=True)
    wo_rows, down_rows = n_u * wo.shape[0], n_u * w_down.shape[0]
    wo_blocks = [wo_all[block_of[z] * wo_rows :][:wo_rows] for z in range(n_z)]
    down_blocks = [down_all[block_of[z] * down_rows :][:down_rows] for z in range(n_z)]

    small = jnp.concatenate([norm1, norm2, segments.reshape(-1).astype(bf16)])[None]
    small = cube_gather(small, ("blk", "ulysses"))
    seg_blocks = (
        small[:, 2 * gain_rows :].astype(jnp.int32).reshape(n_u * n_z, batch_count, tok_rows)
    )
    seq_seg = seg_blocks.transpose(1, 0, 2).reshape(batch_count, seq_len)
    small = cube_gather(small, ("dp",))
    gain1 = small[:, :gain_rows].reshape(1, width).astype(f32)
    gain2 = small[:, gain_rows : 2 * gain_rows].reshape(1, width).astype(f32)

    slots = jnp.arange(n_z, dtype=jnp.int32)
    slot_z = jnp.stack([(z_id - direction_of(m) * slots) % n_z for m in range(batch_count)])
    in_part = (
        slot_z[:, :, None] * tok_rows + jnp.arange(tok_rows, dtype=jnp.int32)[None, None, :]
    ).reshape(batch_count, part_len)
    index = u_id * part_len + in_part
    chosen = (
        (u_id * n_z + slot_z)[:, :, None] == jnp.arange(n_u * n_z, dtype=jnp.int32)[None, None, :]
    ).astype(jnp.int32)
    own_seg = jnp.sum(
        chosen[:, :, :, None] * seq_seg.reshape(batch_count, 1, n_u * n_z, tok_rows), axis=2
    ).reshape(batch_count, part_len)
    start = jnp.sum((seq_seg[:, None, :] < own_seg[:, :, None]).astype(jnp.int32), axis=2)
    position = (index - start).reshape(group_rows)
    half = HD // 2
    inverse_freq = rope_base ** (-2.0 * jnp.arange(half, dtype=f32) / HD)
    angles = position.astype(f32)[:, None] * inverse_freq[None, :]
    cosine, sine = lax.optimization_barrier((jnp.cos(angles), jnp.sin(angles)))
    turning = (q_width + kv_width) // HD
    cos_all = jnp.concatenate(
        [cosine, cosine] * turning + [jnp.ones((group_rows, kv_width), f32)], axis=1
    )
    sin_all = jnp.concatenate(
        [-sine, sine] * turning + [jnp.zeros((group_rows, kv_width), f32)], axis=1
    )
    cos_all, sin_all = lax.optimization_barrier((cos_all, sin_all))
    key_index = jnp.concatenate(
        [index] + [((u_id - step) % n_u) * part_len + in_part for step in range(1, n_u)], axis=1
    )
    start_col, index_col, key_row = start[:, :, None], index[:, :, None], key_index[:, None, :]

    def batches(array):
        return [array[m * part_len : (m + 1) * part_len] for m in range(batch_count)]

    def gathered(array):
        return jnp.concatenate(ring_gather([array[m] for m in range(batch_count)]), axis=0)

    def scattered(partial):
        return jnp.stack(ring_scatter(batches(partial), tok_rows))

    group_tokens = gathered(tokens)
    group_floats = group_tokens.astype(f32)
    unit1_group = group_floats * inverse_norm(group_floats)
    normed1 = (unit1_group * gain1).astype(bf16)
    qkv = turn(matmul(normed1, qkv_w), cos_all, sin_all, 1.0)
    qkv = qkv.reshape(batch_count, part_len, q_width + 2 * kv_width)
    queries = qkv[:, :, :q_width]
    own_kv = qkv[:, :, q_width:]
    kv_parts = [own_kv]
    for step in range(1, n_u):
        kv_parts.append(
            lax.ppermute(own_kv, "ulysses", [(i, i + step) for i in range(n_u - step)])
        )
    all_kv = jnp.concatenate(kv_parts, axis=1)
    keys, values = all_kv[:, :, :kv_width], all_kv[:, :, kv_width:]
    heads = q_width // HD
    products = 2 * batch_count * heads * part_len * seq_len * HD
    exps = batch_count * heads * part_len * seq_len
    attended, log_sums = attend_call(
        functools.partial(attend_kernel, group),
        (queries, keys, values, start_col, index_col, key_row),
        (
            jax.ShapeDtypeStruct(queries.shape, bf16),
            jax.ShapeDtypeStruct((batch_count, part_len, heads), f32),
        ),
        2 * products,
        exps,
    )
    attended = attended.reshape(group_rows, q_width)
    mixed = jnp.concatenate([matmul(attended, block) for block in wo_blocks], axis=1)
    floats = tokens.astype(f32)
    middle = floats + scattered(mixed)
    inverse2 = inverse_norm(middle)
    unit2 = middle * inverse2
    normed2 = gathered((unit2 * gain2[None]).astype(bf16))
    group_cotan = gathered(cotangent)
    gate_proj = matmul(normed2, gate_w)
    up_proj = matmul(normed2, up_w)
    hidden = (jax.nn.silu(gate_proj) * up_proj).astype(bf16)
    ffn = jnp.concatenate([matmul(hidden, block) for block in down_blocks], axis=1)
    result = (middle + scattered(ffn)).astype(bf16)

    cotan_cols = [group_cotan[:, z * w_down.shape[1] :][:, : w_down.shape[1]] for z in range(n_z)]
    grad_hidden = sum(matmul_nt(cotan_cols[z], down_blocks[z]) for z in range(n_z))
    gate_sigmoid = jax.nn.sigmoid(gate_proj)
    grad_gate = (
        grad_hidden * up_proj * gate_sigmoid * (1.0 + gate_proj * (1.0 - gate_sigmoid))
    ).astype(bf16)
    grad_up = (grad_hidden * gate_proj * gate_sigmoid).astype(bf16)
    order = sorted(range(n_z), key=lambda z: block_of[z])

    def reduced(grads):
        return lax.psum_scatter(grads, outer, scatter_dimension=0, tiled=True)

    def returned(grads):
        return lax.ppermute(reduced(grads), ("dp", "blk"), cross_back_pairs(n_z))

    down_grad = returned(
        jnp.concatenate([grad_of(hidden, cotan_cols[z]) for z in order], axis=0)
    )
    gate_grad = reduced(grad_of(normed2, grad_gate))
    up_grad = reduced(grad_of(normed2, grad_up))
    grad_normed2 = scattered(matmul_nt(grad_gate, gate_w) + matmul_nt(grad_up, up_w))
    grad_middle = cotangent.astype(f32) + norm_back(grad_normed2, gain2[None], unit2, inverse2)
    grad_attn = gathered(grad_middle.astype(bf16))
    attn_cols = [grad_attn[:, z * wo.shape[1] :][:, : wo.shape[1]] for z in range(n_z)]
    wo_grad = returned(jnp.concatenate([grad_of(attended, attn_cols[z]) for z in order], axis=0))
    grad_attended = sum(matmul_nt(attn_cols[z], wo_blocks[z]) for z in range(n_z)).astype(bf16)
    grad_q, grad_k, grad_v = attend_call(
        functools.partial(attend_back_kernel, group),
        (
            queries,
            keys,
            values,
            start_col,
            index_col,
            key_row,
            log_sums,
            grad_attended.reshape(queries.shape),
        ),
        (
            jax.ShapeDtypeStruct(queries.shape, f32),
            jax.ShapeDtypeStruct(keys.shape, f32),
            jax.ShapeDtypeStruct(values.shape, f32),
        ),
        5 * products,
        exps,
    )
    grad_kv = jnp.concatenate([grad_k, grad_v], axis=2)
    own_grad_kv = grad_kv[:, :part_len]
    for step in range(1, n_u):
        arrived = lax.ppermute(
            grad_kv[:, step * part_len : (step + 1) * part_len].astype(bf16),
            "ulysses",
            [(i + step, i) for i in range(n_u - step)],
        )
        own_grad_kv = own_grad_kv + arrived.astype(f32)
    grad_qkv = jnp.concatenate([grad_q, own_grad_kv], axis=2).reshape(
        group_rows, q_width + 2 * kv_width
    )
    grad_qkv = turn(grad_qkv, cos_all, sin_all, -1.0)
    qkv_grad = reduced(grad_of(normed1, grad_qkv))
    partial1 = matmul_nt(grad_qkv, qkv_w)
    grad_normed1 = scattered(partial1)
    inverse1 = inverse_norm(floats)
    grad_input = grad_middle + norm_back(grad_normed1, gain1[None], floats * inverse1, inverse1)
    gain_grads = jnp.stack(
        [
            jnp.sum(unit1_group * partial1, axis=0),
            jnp.sum(unit2 * grad_normed2, axis=(0, 1)),
        ],
        axis=1,
    )
    gain_grads = cube_scatter(gain_grads, ("dp", "ulysses", "blk"))
    qkv_grad = qkv_grad.astype(f32)
    return (
        result,
        grad_input,
        gain_grads[:, 0],
        qkv_grad[:, :q_width],
        qkv_grad[:, q_width : q_width + kv_width],
        qkv_grad[:, q_width + kv_width :],
        wo_grad.astype(f32),
        gain_grads[:, 1],
        gate_grad.astype(f32),
        up_grad.astype(f32),
        down_grad.astype(f32),
    )


def splits_evenly(mesh):
    sizes = [mesh.shape[name] for name in ("dp", "ulysses", "blk")]
    return mesh.shape["dp"] == mesh.shape["blk"] and all(size & (size - 1) == 0 for size in sizes)


def solution(mesh):
    in_specs = (
        P(None, ("dp", "ulysses", "blk"), None),
        P(None, ("dp", "ulysses", "blk")),
        P(("dp", "ulysses", "blk")),
        P(("dp", "ulysses"), "blk"),
        P(("dp", "ulysses"), "blk"),
        P(("dp", "ulysses"), "blk"),
        P(("dp", "ulysses"), "blk"),
        P(("dp", "ulysses", "blk")),
        P(("dp", "ulysses"), "blk"),
        P(("dp", "ulysses"), "blk"),
        P(("dp", "ulysses"), "blk"),
        P(None, ("dp", "ulysses", "blk"), None),
    )
    out_specs = (
        P(None, ("dp", "ulysses", "blk"), None),
        P(None, ("dp", "ulysses", "blk"), None),
        P(("dp", "ulysses", "blk")),
        P(("dp", "ulysses"), "blk"),
        P(("dp", "ulysses"), "blk"),
        P(("dp", "ulysses"), "blk"),
        P(("dp", "ulysses"), "blk"),
        P(("dp", "ulysses", "blk")),
        P(("dp", "ulysses"), "blk"),
        P(("dp", "ulysses"), "blk"),
        P(("dp", "ulysses"), "blk"),
    )
    body = split_shards if splits_evenly(mesh) else shards
    return jax.shard_map(body, mesh=mesh, in_specs=in_specs, out_specs=out_specs, check_vma=False)
```
